512 devices in a mesh: leaf: 128 (over y, z_lo, x, core), rank: 4 (over z_hi).
Axes of the slice: x: 4, y: 4, z: 16 (z_hi: 4, z_lo: 4; z = z_hi * 4 + z_lo), core: 2. Of those that a mesh axis runs over, the one named last changes fastest.
Arguments:
- load_vectors: bfloat16 [512, 4, 256], P('leaf'), may hold values from -6 to 6
- cluster_order: int32 [512, 256], P('leaf'), may hold values from 0 to 255, each once within a row
- block_present: int32 [8, 512], P(None, 'leaf'), may hold values 0 or 1
- factors: bfloat16 [8, 512, 2, 256, 256], P(None, 'leaf', None, 'rank'), may hold values from -0.25 to 0.25
Outputs:
- applied: float32 [512, 4, 256], P('leaf')
The draws below stay inside these ranges and needn't reach their ends.
Inputs may be any that keep to these rules, and one draw needn't show every extreme that they name: `cluster_order`: each row is a permutation of 0 .. 255.
All inputs are finite; a program needn't handle non-finite values. No bound on the sum of `block_present` on one device may be relied on, other than what follows from the above.
Results may differ from the reference program's by a relative error of at most 0.012.
Values may be sent and summed in bfloat16 or wider, within the bound.
No kernel may reach another device: no remote copies, remote signals or barrier semaphores. Data moves between devices by JAX's collectives and lax.ppermute only.
A program may use at most 64 MiB of HBM per device.

```python
import jax
import jax.numpy as jnp
from jax import lax

B = 256
LOADS = 4
LEVELS = 8
BLOCKS = 512


def place_ends(result, stream_key, least, largest):
    extent = result.shape
    index_at = [jax.random.randint(jax.random.fold_in(stream_key, axis), (), 0, extent[axis]) for axis in range(len(extent))]
    result = result.at[tuple(index_at)].set(least)
    longest = extent.index(max(extent))
    index_at[longest] = (index_at[longest] + 1) % extent[longest]
    return result.at[tuple(index_at)].set(largest)


def levels(key, shape, cuts, smallest, largest):
    gain = 1.0
    for axis_at, parts in cuts:
        steps = jax.random.uniform(jax.random.fold_in(jax.random.fold_in(key, 6), axis_at), (parts,), jnp.float32, smallest / len(cuts), largest / len(cuts))
        gain = gain * jnp.repeat(jnp.exp(steps), shape[axis_at] // parts).reshape((-1,) + (1,) * (len(shape) - 1 - axis_at))
    return gain


def gaussian(rng, extent, spread, reach, shards=(), kind=jnp.bfloat16):
    gain = levels(rng, extent, shards, -0.22, 0.18) if shards else 1.0
    entries = jax.random.normal(rng, extent, jnp.float32) * spread * gain
    return jnp.minimum(jnp.maximum(entries, -reach), reach).astype(kind)


def setup_inputs(seed: int = 0) -> dict:
    seeds = jax.random.split(jax.random.key(seed), 5)
    load_vectors = gaussian(seeds[0], (BLOCKS, LOADS, B), 1.0, 6.0, ((0, 128),))
    cluster_order = jax.vmap(lambda own: jax.random.permutation(own, B))(jax.random.split(seeds[1], BLOCKS)).reshape((BLOCKS, B)).astype(jnp.int32)
    block_present = place_ends((jax.random.randint(seeds[2], (LEVELS, BLOCKS), 0, 4) < 3).astype(jnp.int32), jax.random.fold_in(seeds[2], 1), 0, 1)
    factors = gaussian(seeds[3], (LEVELS, BLOCKS, 2, B, B), (2 * B) ** -0.5, 0.25, ((1, 128), (3, 4)))
    return dict(load_vectors=load_vectors, cluster_order=cluster_order, block_present=block_present, factors=factors)


def reference(load_vectors, cluster_order, block_present, factors):
    current = jnp.take_along_axis(load_vectors, cluster_order[:, None, :], axis=2).astype(jnp.float32)
    tree_bits = BLOCKS.bit_length() - 1
    block_ids = jnp.arange(BLOCKS, dtype=jnp.int32)
    for level_idx in range(LEVELS):
        level_bit = (tree_bits - 1 - level_idx) % tree_bits
        rounded = lax.optimization_barrier(current.astype(jnp.bfloat16)).astype(jnp.float32)
        partner = rounded[block_ids ^ (1 << level_bit)]
        weights = factors[level_idx].astype(jnp.float32)
        own_term = jnp.einsum("blc,bco->blo", rounded, weights[:, 0], precision=lax.Precision.HIGHEST)
        off_term = jnp.einsum("blc,bco->blo", partner, weights[:, 1], precision=lax.Precision.HIGHEST)
        current = own_term + block_present[level_idx].astype(jnp.float32)[:, None, None] * off_term
    inverse = jnp.argsort(cluster_order, axis=1).astype(jnp.int32)
    return jnp.take_along_axis(current, inverse[:, None, :], axis=2)
```

```python
import jax
import jax.numpy as jnp
from jax import lax
from jax.sharding import PartitionSpec as P

LEVELS = 8
F32 = jnp.float32
BF16 = jnp.bfloat16


def left_half():
    return lax.broadcasted_iota(jnp.int32, (8, 128), 1) < 64


def turned(tile):
    return jnp.concatenate([tile[:, 64:], tile[:, :64]], axis=1)


def own_columns(loads, order, rank):
    quarter = lax.dynamic_slice_in_dim(order, 64 * rank, 64, 1)
    pick = (jnp.arange(256)[None, :, None] == quarter[:, None, :]).astype(BF16)
    got = jnp.einsum("blc,bco->blo", loads, pick, preferred_element_type=F32)
    return jnp.concatenate([got[:2].reshape(8, 64), got[2:].reshape(8, 64)], axis=1)


def product(own, partner, mask, weights):
    left = left_half()
    top = jnp.where(left, own, turned(partner))
    bottom = jnp.where(left, turned(own), partner)
    cols = jnp.concatenate([top, bottom], axis=0).astype(BF16)
    wide = jnp.concatenate([cols] * 4, axis=1) * mask
    return jnp.dot(wide, weights, preferred_element_type=F32)


def chunks(part, copies):
    left = left_half()
    pieces = []
    for at in range(2):
        tile = part[:, 128 * at : 128 * (at + 1)]
        top, bottom = tile[:8], tile[8:]
        pieces += [jnp.where(left, top, turned(bottom)), jnp.where(left, turned(top), bottom)]
    return jnp.broadcast_to(jnp.stack(pieces)[None], (copies, 4, 8, 128)).reshape(copies * 4, 8, 128)


def put_back(state, order):
    high = state.astype(BF16)
    rest = state - high.astype(F32)
    middle = rest.astype(BF16)
    low = (rest - middle.astype(F32)).astype(BF16)
    pieces = jnp.concatenate([high, middle, low], axis=0).reshape(3, 4, 4, 256)
    pick = (jnp.arange(256)[None, :, None] == order[:, None, :]).astype(BF16)
    put = jnp.einsum("pblj,bij->pbli", pieces, pick, preferred_element_type=F32)
    return put[0] + put[1] + put[2]


def pair_groups(leaves, ranks, bit):
    groups = []
    for leaf in range(leaves):
        if not leaf >> bit & 1:
            groups.append([at * ranks + r for at in (leaf, leaf | 1 << bit) for r in range(ranks)])
    return groups


def masks(present):
    block_of = jnp.arange(16) // 4
    wide = jnp.arange(512)
    same = block_of[:, None] == (wide // 128)[None, :]
    own = (wide % 128 < 64)[None, None, :]
    there = jnp.repeat(present, 4, axis=1)[:, :, None] != 0
    return jnp.where(same[None] & (own | there), 1.0, 0.0).astype(BF16)


def local(load_vectors, cluster_order, block_present, factors):
    leaves, ranks = lax.axis_size("leaf"), lax.axis_size("rank")
    leaf_bits = leaves.bit_length() - 1
    leaf, rank = lax.axis_index("leaf"), lax.axis_index("rank")
    weights = factors.reshape(LEVELS, 512, 256)
    mask = masks(block_present)
    own = own_columns(load_vectors, cluster_order, rank)
    partner = lax.ppermute(own, "leaf", [(at, at ^ 1 << leaf_bits - 1) for at in range(leaves)])
    uppers = [(leaf >> bit & 1) != 0 for bit in range(leaf_bits - 1)]
    partner, *uppers = lax.optimization_barrier((partner, *uppers))
    for level in range(LEVELS):
        part = product(own, partner, mask[level], weights[level])
        bit = leaf_bits - 2 - level
        if bit >= 0:
            received = lax.all_to_all(
                chunks(part, 2), ("leaf", "rank"), 0, 0, axis_index_groups=pair_groups(leaves, ranks, bit), tiled=True
            )
            upper = uppers[bit]
            low, high = received[:4].sum(0), received[4:].sum(0)
            own = jnp.where(upper, high, low)
            partner = jnp.where(upper, low, high)
        elif level < LEVELS - 1:
            own = lax.all_to_all(chunks(part, 1), "rank", 0, 0, tiled=True).sum(0)
            partner = turned(own)
    whole = lax.all_to_all(jnp.stack([part] * ranks), "rank", 0, 0, tiled=True).sum(0)
    return put_back(whole, cluster_order)


def solution(mesh):
    in_specs = (
        P("leaf", None, None),
        P("leaf", None),
        P(None, "leaf"),
        P(None, "leaf", None, "rank", None),
    )
    out_specs = P("leaf", None, None)
    return jax.shard_map(local, mesh=mesh, in_specs=in_specs, out_specs=out_specs, check_vma=False)
```

```python
import jax
import jax.numpy as jnp
from jax import lax
from jax.sharding import PartitionSpec as P

LEVELS = 8
F32 = jnp.float32
BF16 = jnp.bfloat16
WIDE = BF16
BY_COLUMNS = (4, 6)


def left_half():
    return lax.broadcasted_iota(jnp.int32, (8, 128), 1) < 64


def turned(tile):
    return jnp.concatenate([tile[:, 64:], tile[:, :64]], axis=1)


def own_columns(loads, order, rank):
    quarter = lax.dynamic_slice_in_dim(order, 64 * rank, 64, 1)
    pick = (jnp.arange(256)[None, :, None] == quarter[:, None, :]).astype(BF16)
    got = jnp.einsum("blc,bco->blo", loads, pick, preferred_element_type=F32)
    return jnp.concatenate([got[:2].reshape(8, 64), got[2:].reshape(8, 64)], axis=1)


def product(own, partner, mask, weights):
    left = left_half()
    top = jnp.where(left, own, turned(partner))
    bottom = jnp.where(left, turned(own), partner)
    cols = jnp.concatenate([top, bottom], axis=0).astype(BF16)
    wide = jnp.concatenate([cols] * 4, axis=1) * mask
    return jnp.dot(wide, weights, preferred_element_type=F32)


def chunks(part, copies):
    left = left_half()
    pieces = []
    for at in range(2):
        tile = part[:, 128 * at : 128 * (at + 1)]
        top, bottom = tile[:8], tile[8:]
        pieces += [jnp.where(left, top, turned(bottom)), jnp.where(left, turned(top), bottom)]
    return jnp.broadcast_to(jnp.stack(pieces)[None], (copies, 4, 8, 128)).reshape(copies * 4, 8, 128)


def put_back(state, order):
    high = state.astype(BF16)
    rest = state - high.astype(F32)
    middle = rest.astype(BF16)
    low = (rest - middle.astype(F32)).astype(BF16)
    pieces = jnp.concatenate([high, middle, low], axis=0).reshape(3, 4, 4, 256)
    pick = (jnp.arange(256)[None, :, None] == order[:, None, :]).astype(BF16)
    put = jnp.einsum("pblj,bij->pbli", pieces, pick, preferred_element_type=F32)
    return put[0] + put[1] + put[2]


def pair_groups(leaves, ranks, bit):
    groups = []
    for leaf in range(leaves):
        if not leaf >> bit & 1:
            groups.append([at * ranks + r for at in (leaf, leaf | 1 << bit) for r in range(ranks)])
    return groups


def masks(present):
    block_of = jnp.arange(16) // 4
    wide = jnp.arange(512)
    same = block_of[:, None] == (wide // 128)[None, :]
    own = (wide % 128 < 64)[None, None, :]
    there = jnp.repeat(present, 4, axis=1)[:, :, None] != 0
    return jnp.where(same[None] & (own | there), 1.0, 0.0).astype(BF16)


def piece_for(pieces, quarter):
    return lax.dynamic_index_in_dim(pieces, quarter, 0, keepdims=False)


def column_pieces(weights):
    parts = [jnp.concatenate([weights[:, 0, :, 64 * q : 64 * q + 64], weights[:, 1, :, 64 * q : 64 * q + 64]], 2) for q in range(4)]
    return jnp.stack(parts)


def assembled(*pieces):
    return jnp.stack([pieces[0], pieces[3], pieces[2], pieces[1]], axis=1).reshape(1024, 128)


def column_product(own, partner, mask, columns, rank):
    both = jnp.concatenate([own, partner], axis=0).astype(BF16)
    turn = lax.dynamic_slice_in_dim(jnp.concatenate([both, both], axis=1), 64 * rank, 256, 1)
    got = jnp.dot(jnp.concatenate([turn] * 4, axis=1) * mask, columns, preferred_element_type=F32)
    got = got[:16, :64] + got[16:, 64:]
    return jnp.concatenate([got[:8], got[8:]], axis=1)


def column_masks(present):
    block_of = jnp.arange(16) // 4
    same = block_of[:, None] == (jnp.arange(1024) // 256)[None, :]
    there = jnp.repeat(present, 4)[:, None] != 0
    return jnp.where(jnp.concatenate([same, same & there], axis=0), 1.0, 0.0).astype(BF16)


def by_side(received, upper):
    low, high = received[:4].astype(F32).sum(0), received[4:].astype(F32).sum(0)
    return jnp.where(upper, high, low), jnp.where(upper, low, high)


def local(load_vectors, cluster_order, block_present, factors):
    leaves, ranks = lax.axis_size("leaf"), lax.axis_size("rank")
    leaf_bits = leaves.bit_length() - 1
    leaf, rank = lax.axis_index("leaf"), lax.axis_index("rank")
    own = own_columns(load_vectors, cluster_order, rank)
    partner = lax.ppermute(own, "leaf", [(at, at ^ 1 << leaf_bits - 1) for at in range(leaves)])
    uppers = [(leaf >> bit & 1) != 0 for bit in range(leaf_bits - 1)]
    early, late = BY_COLUMNS
    pieces = column_pieces(factors[early])
    ahead = jnp.stack([piece_for(pieces, rank + step & ranks - 1) for step in (1, 2)])
    mask_first = masks(block_present[:1])[0]
    partner, ahead, *uppers = lax.optimization_barrier((partner, ahead, *uppers))
    forward = [(r, (r + 1) % ranks) for r in range(ranks)]
    backward = [(r, (r - 1) % ranks) for r in range(ranks)]
    columns = {}

    for level in range(LEVELS):
        bit = leaf_bits - 2 - level
        groups = pair_groups(leaves, ranks, bit) if bit >= 0 else None
        if level in BY_COLUMNS:
            own = column_product(whole_own, whole_partner, both_masks[level], columns[level], rank)
            if bit >= 0:
                partner = lax.ppermute(own.astype(BF16), "leaf", [(at, at ^ 1 << bit) for at in range(leaves)])
                partner = partner.astype(F32)
            else:
                partner = turned(own)
            continue
        if level == 0:
            part = product(own, partner, mask_first, factors[0].reshape(512, 256))
            part, block_present, factors = lax.optimization_barrier((part, block_present, factors))
            mask = masks(block_present)
            weights = factors.reshape(LEVELS, 512, 256)
            moved = {
                at: [piece_for(column_pieces(factors[at]), rank + step & ranks - 1) for step in range(ranks)]
                for at in BY_COLUMNS
            }
            both_masks = {at: column_masks(block_present[at]) for at in BY_COLUMNS}
        else:
            part = product(own, partner, mask[level], weights[level])
        if level < 4:
            if level == 0:
                first = lax.ppermute(ahead, "rank", forward)
            elif level == 1:
                second = lax.ppermute(jnp.stack([moved[early][3], moved[late][2]]), "rank", backward)
            elif level == 2:
                third = lax.ppermute(jnp.stack([first[1], moved[late][1]]), "rank", forward)
            else:
                fourth = lax.ppermute(jnp.stack([second[1], moved[late][3]]), "rank", backward)
        if level == 3:
            part, mine, near, other = lax.optimization_barrier((part, moved[early][0], first[0], second[0]))
            columns[early] = assembled(mine, near, third[0], other)
        elif level == 5:
            part, mine, near, far, other = lax.optimization_barrier(
                (part, moved[late][0], third[1], fourth[0], fourth[1])
            )
            columns[late] = assembled(mine, near, far, other)
        if level + 1 in BY_COLUMNS:
            sent = jnp.broadcast_to(part.astype(WIDE)[None], (2 * ranks, 16, 256))
            received = lax.all_to_all(sent, ("leaf", "rank"), 0, 0, axis_index_groups=groups, tiled=True)
            whole_own, whole_partner = by_side(received, uppers[bit])
        elif bit >= 0:
            received = lax.all_to_all(chunks(part, 2), ("leaf", "rank"), 0, 0, axis_index_groups=groups, tiled=True)
            own, partner = by_side(received, uppers[bit])
        elif level < LEVELS - 1:
            own = lax.all_to_all(chunks(part, 1), "rank", 0, 0, tiled=True).sum(0)
            partner = turned(own)
        else:
            sent = jnp.broadcast_to(part.astype(WIDE)[None], (ranks, 16, 256))
            whole = lax.all_to_all(sent, "rank", 0, 0, tiled=True).astype(F32).sum(0)
    return put_back(whole, cluster_order)


def solution(mesh):
    in_specs = (
        P("leaf", None, None),
        P("leaf", None),
        P(None, "leaf"),
        P(None, "leaf", None, "rank", None),
    )
    out_specs = P("leaf", None, None)

    return jax.shard_map(local, mesh=mesh, in_specs=in_specs, out_specs=out_specs, check_vma=False)
```

```python
import jax
import jax.numpy as jnp
from jax import lax
from jax.sharding import PartitionSpec as P

LEVELS = 8
F32 = jnp.float32
BF16 = jnp.bfloat16
WIDE = BF16
BY_COLUMNS = (3, 6)


def left_half():
    return lax.broadcasted_iota(jnp.int32, (8, 128), 1) < 64


def turned(tile):
    return jnp.concatenate([tile[:, 64:], tile[:, :64]], axis=1)


def own_columns(loads, order, rank):
    quarter = lax.dynamic_slice_in_dim(order, 64 * rank, 64, 1)
    pick = (jnp.arange(256)[None, :, None] == quarter[:, None, :]).astype(BF16)
    got = jnp.einsum("blc,bco->blo", loads, pick, preferred_element_type=F32)
    return jnp.concatenate([got[:2].reshape(8, 64), got[2:].reshape(8, 64)], axis=1)


def per_block(wide):
    _, columns = wide.shape
    block_of = lax.broadcasted_iota(jnp.int32, wide.shape, 0) // 4 % 4
    part_of = lax.broadcasted_iota(jnp.int32, wide.shape, 1) // (columns // 4)
    return jnp.where(block_of == part_of, wide, jnp.zeros((), wide.dtype))


def product(own, partner, present, weights):
    left = left_half()
    partner = partner * present
    top = jnp.where(left, own, turned(partner))
    bottom = jnp.where(left, turned(own), partner)
    cols = jnp.concatenate([top, bottom], axis=0).astype(BF16)
    wide = per_block(jnp.concatenate([cols] * 4, axis=1))
    return jnp.dot(wide, weights, preferred_element_type=F32)


def chunks(part, copies):
    left = left_half()
    pieces = []
    for at in range(2):
        tile = part[:, 128 * at : 128 * (at + 1)]
        top, bottom = tile[:8], tile[8:]
        pieces += [jnp.where(left, top, turned(bottom)), jnp.where(left, turned(top), bottom)]
    return jnp.broadcast_to(jnp.stack(pieces)[None], (copies, 4, 8, 128)).reshape(copies * 4, 8, 128)


def put_back(state, order):
    high = state.astype(BF16)
    rest = state - high.astype(F32)
    middle = rest.astype(BF16)
    low = (rest - middle.astype(F32)).astype(BF16)
    pieces = jnp.concatenate([high, middle, low], axis=0).reshape(3, 4, 4, 256)
    pick = (jnp.arange(256)[None, :, None] == order[:, None, :]).astype(BF16)
    put = jnp.einsum("pblj,bij->pbli", pieces, pick, preferred_element_type=F32)
    return put[0] + put[1] + put[2]


def pair_groups(leaves, ranks, bit):
    groups = []
    for leaf in range(leaves):
        if not leaf >> bit & 1:
            groups.append([at * ranks + r for at in (leaf, leaf | 1 << bit) for r in range(ranks)])
    return groups


def present_tiles(present):
    levels = present.shape[0]
    spread = present.reshape(levels, 2, 2).transpose(0, 2, 1).astype(F32)
    return jnp.broadcast_to(spread[:, :, None, :, None], (levels, 2, 4, 2, 64)).reshape(levels, 8, 128)


def piece_for(pieces, quarter):
    return lax.dynamic_index_in_dim(pieces, quarter, 0, keepdims=False)


def column_pieces(weights):
    parts = [jnp.concatenate([weights[:, 0, :, 64 * q : 64 * q + 64], weights[:, 1, :, 64 * q : 64 * q + 64]], 2) for q in range(4)]
    return jnp.stack(parts)


def assembled(mine, first, second, far, first_is_next):
    after, before = jnp.where(first_is_next, first, second), jnp.where(first_is_next, second, first)
    return jnp.stack([mine, after, far, before], axis=1).reshape(1024, 128)


def column_product(own, partner, present, columns, rank):
    partner = partner * jnp.repeat(present.astype(F32), 4)[:, None]
    both = jnp.concatenate([own, partner], axis=0).astype(BF16)
    turn = lax.dynamic_slice_in_dim(jnp.concatenate([both, both], axis=1), 64 * rank, 256, 1)
    got = jnp.dot(per_block(jnp.concatenate([turn] * 4, axis=1)), columns, preferred_element_type=F32)
    got = got[:16, :64] + got[16:, 64:]
    return jnp.concatenate([got[:8], got[8:]], axis=1)


def by_side(received, upper):
    low, high = received[:4].astype(F32).sum(0), received[4:].astype(F32).sum(0)
    return jnp.where(upper, high, low), jnp.where(upper, low, high)


def local(load_vectors, cluster_order, block_present, factors):
    leaves, ranks = lax.axis_size("leaf"), lax.axis_size("rank")
    leaf_bits = leaves.bit_length() - 1
    leaf, rank = lax.axis_index("leaf"), lax.axis_index("rank")
    own = own_columns(load_vectors, cluster_order, rank)
    partner = lax.ppermute(own, "leaf", [(at, at ^ 1 << leaf_bits - 1) for at in range(leaves)])
    uppers = [(leaf >> bit & 1) != 0 for bit in range(leaf_bits - 1)]
    core = leaf & 1
    steps = (jnp.where(core == 0, rank ^ 1, 3 - rank), jnp.where(core == 0, 3 - rank, rank ^ 1))

    def moved_on(pieces, step):
        route = []
        for at in range(leaves):
            for r in range(ranks):
                route.append((at * ranks + r, at * ranks + (r ^ 1 if at & 1 == step else 3 - r)))
        return lax.ppermute(jnp.stack(pieces), ("leaf", "rank"), route)

    early, late = BY_COLUMNS
    pieces = {level: column_pieces(factors[level]) for level in BY_COLUMNS}
    moved = [piece_for(pieces[level], to) for level in BY_COLUMNS for to in (rank, *steps, rank ^ 2)]
    first_is_next = (rank + core & 1) == 0
    tiles = present_tiles(block_present)
    partner, tiles, block_present, *rest = lax.optimization_barrier((partner, tiles, block_present, *moved, *uppers))
    of_early, of_late, uppers = rest[:ranks], rest[ranks : 2 * ranks], rest[2 * ranks :]
    columns = {}

    for level in range(LEVELS):
        bit = leaf_bits - 2 - level
        groups = pair_groups(leaves, ranks, bit) if bit >= 0 else None
        if level == early:
            second, whole_own, whole_partner = lax.optimization_barrier((second, whole_own, whole_partner))
            columns[early] = assembled(of_early[0], first[0], second[0], second[1], first_is_next)
        elif level == late:
            third, whole_own, whole_partner = lax.optimization_barrier((third, whole_own, whole_partner))
            columns[late] = assembled(of_late[0], first[2], third[0], third[1], first_is_next)
        if level in BY_COLUMNS:
            own = column_product(whole_own, whole_partner, block_present[level], columns[level], rank)
            if bit >= 0:
                partner = lax.ppermute(own.astype(BF16), "leaf", [(at, at ^ 1 << bit) for at in range(leaves)])
                partner = partner.astype(F32)
            else:
                partner = turned(own)
            continue
        part, factors = lax.optimization_barrier(
            (product(own, partner, tiles[level], factors[level].reshape(512, 256)), factors)
        )
        if level == 0:
            first = moved_on([of_early[1], of_early[3], of_late[1], of_late[3]], 0)
        elif level == 1:
            second = moved_on([of_early[2], first[1]], 1)
        elif level == 4:
            third = moved_on([of_late[2], first[3]], 1)
        if level + 1 in BY_COLUMNS:
            sent = jnp.broadcast_to(part.astype(WIDE)[None], (2 * ranks, 16, 256))
            received = lax.all_to_all(sent, ("leaf", "rank"), 0, 0, axis_index_groups=groups, tiled=True)
            whole_own, whole_partner = by_side(received, uppers[bit])
        elif bit >= 0:
            received = lax.all_to_all(chunks(part, 2), ("leaf", "rank"), 0, 0, axis_index_groups=groups, tiled=True)
            own, partner = by_side(received, uppers[bit])
        elif level < LEVELS - 1:
            own = lax.all_to_all(chunks(part, 1), "rank", 0, 0, tiled=True).sum(0)
            partner = turned(own)
        else:
            sent = jnp.broadcast_to(part.astype(WIDE)[None], (ranks, 16, 256))
            whole = lax.all_to_all(sent, "rank", 0, 0, tiled=True).astype(F32).sum(0)
    return put_back(whole, cluster_order)


def solution(mesh):
    in_specs = (
        P("leaf", None, None),
        P("leaf", None),
        P(None, "leaf"),
        P(None, "leaf", None, "rank", None),
    )
    out_specs = P("leaf", None, None)

    return jax.shard_map(local, mesh=mesh, in_specs=in_specs, out_specs=out_specs, check_vma=False)
```

```python
import jax
import jax.numpy as jnp
from jax import lax
from jax.sharding import PartitionSpec as P

LEVELS = 8
F32 = jnp.float32
BF16 = jnp.bfloat16
WIDE = BF16
BY_COLUMNS = (3, 6)


def left_half():
    return lax.broadcasted_iota(jnp.int32, (8, 128), 1) < 64


def turned(tile):
    return jnp.concatenate([tile[:, 64:], tile[:, :64]], axis=1)


def own_columns(loads, order, rank):
    quarter = lax.dynamic_slice_in_dim(order, 64 * rank, 64, 1)
    pick = (jnp.arange(256)[None, :, None] == quarter[:, None, :]).astype(BF16)
    got = jnp.einsum("blc,bco->blo", loads, pick, preferred_element_type=F32)
    return jnp.concatenate([got[:2].reshape(8, 64), got[2:].reshape(8, 64)], axis=1)


def per_block(wide):
    _, columns = wide.shape
    block_of = lax.broadcasted_iota(jnp.int32, wide.shape, 0) // 4 % 4
    part_of = lax.broadcasted_iota(jnp.int32, wide.shape, 1) // (columns // 4)
    return jnp.where(block_of == part_of, wide, jnp.zeros((), wide.dtype))


def product(own, partner, present, weights):
    left = left_half()
    partner = partner * present
    top = jnp.where(left, own, turned(partner))
    bottom = jnp.where(left, turned(own), partner)
    cols = jnp.concatenate([top, bottom], axis=0).astype(BF16)
    wide = per_block(jnp.concatenate([cols] * 4, axis=1))
    return jnp.dot(wide, weights, preferred_element_type=F32)


def chunks(part, copies):
    left = left_half()
    pieces = []
    for at in range(2):
        tile = part[:, 128 * at : 128 * (at + 1)]
        top, bottom = tile[:8], tile[8:]
        pieces += [jnp.where(left, top, turned(bottom)), jnp.where(left, turned(top), bottom)]
    return jnp.broadcast_to(jnp.stack(pieces)[None], (copies, 4, 8, 128)).reshape(copies * 4, 8, 128)


def put_back(state, order):
    high = state.astype(BF16)
    rest = state - high.astype(F32)
    middle = rest.astype(BF16)
    low = (rest - middle.astype(F32)).astype(BF16)
    pieces = jnp.concatenate([high, middle, low], axis=0).reshape(3, 4, 4, 256)
    pick = (jnp.arange(256)[None, :, None] == order[:, None, :]).astype(BF16)
    put = jnp.einsum("pblj,bij->pbli", pieces, pick, preferred_element_type=F32)
    return put[0] + put[1] + put[2]


def pair_groups(leaves, ranks, bit):
    groups = []
    for leaf in range(leaves):
        if not leaf >> bit & 1:
            groups.append([at * ranks + r for at in (leaf, leaf | 1 << bit) for r in range(ranks)])
    return groups


def present_tiles(present):
    levels = present.shape[0]
    spread = present.reshape(levels, 2, 2).transpose(0, 2, 1).astype(F32)
    return jnp.broadcast_to(spread[:, :, None, :, None], (levels, 2, 4, 2, 64)).reshape(levels, 8, 128)


def piece_for(pieces, quarter):
    return lax.dynamic_index_in_dim(pieces, quarter, 0, keepdims=False)


def column_pieces(weights):
    parts = [jnp.concatenate([weights[:, 0, :, 64 * q : 64 * q + 64], weights[:, 1, :, 64 * q : 64 * q + 64]], 2) for q in range(4)]
    return jnp.stack(parts)


def assembled(mine, first, second, far, first_is_next):
    after, before = jnp.where(first_is_next, first, second), jnp.where(first_is_next, second, first)
    return jnp.stack([mine, after, far, before], axis=1).reshape(1024, 128)


def column_product(own, partner, present, columns, start, keep):
    both = jnp.concatenate([own, partner * present], axis=0).astype(BF16)
    turn = lax.dynamic_slice(jnp.concatenate([both, both], axis=1), (jnp.uint32(0), start), (32, 256))
    wide = jnp.where(keep, jnp.concatenate([turn] * 4, axis=1), jnp.zeros((), BF16))
    got = jnp.dot(wide, columns, preferred_element_type=F32)
    got = got[:16, :64] + got[16:, 64:]
    return jnp.concatenate([got[:8], got[8:]], axis=1)


def by_side(received, upper):
    low, high = received[:4].astype(F32).sum(0), received[4:].astype(F32).sum(0)
    return jnp.where(upper, high, low), jnp.where(upper, low, high)


def local(load_vectors, cluster_order, block_present, factors):
    leaves, ranks = lax.axis_size("leaf"), lax.axis_size("rank")
    leaf_bits = leaves.bit_length() - 1
    leaf, rank = lax.axis_index("leaf"), lax.axis_index("rank")
    own = own_columns(load_vectors, cluster_order, rank)
    partner = lax.ppermute(own, "leaf", [(at, at ^ 1 << leaf_bits - 1) for at in range(leaves)])
    uppers = [(leaf >> bit & 1) != 0 for bit in range(leaf_bits - 1)]
    core = leaf & 1
    steps = (jnp.where(core == 0, rank ^ 1, 3 - rank), jnp.where(core == 0, 3 - rank, rank ^ 1))

    def moved_on(pieces, step):
        route = []
        for at in range(leaves):
            for r in range(ranks):
                route.append((at * ranks + r, at * ranks + (r ^ 1 if at & 1 == step else 3 - r)))
        return lax.ppermute(jnp.stack(pieces), ("leaf", "rank"), route)

    early, late = BY_COLUMNS
    pieces = {level: column_pieces(factors[level]) for level in BY_COLUMNS}
    moved = [piece_for(pieces[level], to) for level in BY_COLUMNS for to in (rank, *steps, rank ^ 2)]
    first_is_next = (rank + core & 1) == 0
    tiles = present_tiles(block_present)
    partner, tiles, block_present, *rest = lax.optimization_barrier((partner, tiles, block_present, *moved, *uppers))
    of_early, of_late, uppers = rest[:ranks], rest[ranks : 2 * ranks], rest[2 * ranks :]
    columns = {}

    for level in range(LEVELS):
        bit = leaf_bits - 2 - level
        groups = pair_groups(leaves, ranks, bit) if bit >= 0 else None
        if level == early:
            second, whole_own, whole_partner = lax.optimization_barrier((second, whole_own, whole_partner))
            columns[early] = assembled(of_early[0], first[0], second[0], second[1], first_is_next)
        elif level == late:
            fourth, whole_own, whole_partner = lax.optimization_barrier((fourth, whole_own, whole_partner))
            columns[late] = assembled(of_late[0], third[0], fourth[0], fourth[1], first_is_next)
        if level in BY_COLUMNS:
            own = column_product(whole_own, whole_partner, rows[level], columns[level], start, keep)
            if bit >= 0:
                partner = lax.ppermute(own.astype(BF16), "leaf", [(at, at ^ 1 << bit) for at in range(leaves)])
                partner = partner.astype(F32)
            else:
                partner = turned(own)
            continue
        part, factors = lax.optimization_barrier(
            (product(own, partner, tiles[level], factors[level].reshape(512, 256)), factors)
        )
        if level == 1:
            rows = [jnp.repeat(block_present[at].astype(F32), 4)[:, None] for at in BY_COLUMNS]
            keep = jnp.arange(32)[:, None] // 4 % 4 == jnp.arange(1024)[None, :] // 256
            part, first_is_next, start, keep, *rows = lax.optimization_barrier(
                (part, first_is_next, (64 * rank).astype(jnp.uint32), keep, *rows)
            )
            rows = dict(zip(BY_COLUMNS, rows))
        if level == 0:
            first = moved_on([of_early[1], of_early[3]], 0)
        elif level == 1:
            second = moved_on([of_early[2], first[1]], 1)
        elif level == 2:
            third = moved_on([of_late[1], of_late[3]], 0)
        elif level == 4:
            fourth = moved_on([of_late[2], third[1]], 1)
        if level + 1 in BY_COLUMNS:
            sent = jnp.broadcast_to(part.astype(WIDE)[None], (2 * ranks, 16, 256))
            received = lax.all_to_all(sent, ("leaf", "rank"), 0, 0, axis_index_groups=groups, tiled=True)
            whole_own, whole_partner = by_side(received, uppers[bit])
        elif bit >= 0:
            received = lax.all_to_all(chunks(part, 2), ("leaf", "rank"), 0, 0, axis_index_groups=groups, tiled=True)
            own, partner = by_side(received, uppers[bit])
        elif level < LEVELS - 1:
            own = lax.all_to_all(chunks(part, 1), "rank", 0, 0, tiled=True).sum(0)
            partner = turned(own)
        else:
            sent = jnp.broadcast_to(part.astype(WIDE)[None], (ranks, 16, 256))
            whole = lax.all_to_all(sent, "rank", 0, 0, tiled=True).astype(F32).sum(0)
    return put_back(whole, cluster_order)


def solution(mesh):
    in_specs = (
        P("leaf", None, None),
        P("leaf", None),
        P(None, "leaf"),
        P(None, "leaf", None, "rank", None),
    )
    out_specs = P("leaf", None, None)

    return jax.shard_map(local, mesh=mesh, in_specs=in_specs, out_specs=out_specs, check_vma=False)
```

```python
import jax
import jax.numpy as jnp
from jax import lax
from jax.sharding import PartitionSpec as P

LEVELS = 8
F32 = jnp.float32
BF16 = jnp.bfloat16
WIDE = BF16
BY_COLUMNS = (3, 6)


def left_half():
    return lax.broadcasted_iota(jnp.int32, (8, 128), 1) < 64


def turned(tile):
    return jnp.concatenate([tile[:, 64:], tile[:, :64]], axis=1)


def own_columns(loads, order, rank):
    quarter = lax.dynamic_slice_in_dim(order, 64 * rank, 64, 1)
    pick = (jnp.arange(256)[None, :, None] == quarter[:, None, :]).astype(BF16)
    got = jnp.einsum("blc,bco->blo", loads, pick, preferred_element_type=F32)
    return jnp.concatenate([got[:2].reshape(8, 64), got[2:].reshape(8, 64)], axis=1)


def per_block(wide):
    _, columns = wide.shape
    block_of = lax.broadcasted_iota(jnp.int32, wide.shape, 0) // 4 % 4
    part_of = lax.broadcasted_iota(jnp.int32, wide.shape, 1) // (columns // 4)
    return jnp.where(block_of == part_of, wide, jnp.zeros((), wide.dtype))


def product(own, partner, present, weights):
    left = left_half()
    partner = partner * present
    top = jnp.where(left, own, turned(partner))
    bottom = jnp.where(left, turned(own), partner)
    cols = jnp.concatenate([top, bottom], axis=0).astype(BF16)
    wide = per_block(jnp.concatenate([cols] * 4, axis=1))
    return jnp.dot(wide, weights, preferred_element_type=F32)


def chunks(part, copies):
    left = left_half()
    pieces = []
    for at in range(2):
        tile = part[:, 128 * at : 128 * (at + 1)]
        top, bottom = tile[:8], tile[8:]
        pieces += [jnp.where(left, top, turned(bottom)), jnp.where(left, turned(top), bottom)]
    return jnp.broadcast_to(jnp.stack(pieces)[None], (copies, 4, 8, 128)).reshape(copies * 4, 8, 128)


def put_back(state, order):
    high = state.astype(BF16)
    rest = state - high.astype(F32)
    middle = rest.astype(BF16)
    low = (rest - middle.astype(F32)).astype(BF16)
    pieces = jnp.concatenate([high, middle, low], axis=0).reshape(3, 4, 4, 256)
    pick = (jnp.arange(256)[None, :, None] == order[:, None, :]).astype(BF16)
    put = jnp.einsum("pblj,bij->pbli", pieces, pick, preferred_element_type=F32)
    return put[0] + put[1] + put[2]


def pair_groups(leaves, ranks, bit):
    groups = []
    for leaf in range(leaves):
        if not leaf >> bit & 1:
            groups.append([at * ranks + r for at in (leaf, leaf | 1 << bit) for r in range(ranks)])
    return groups


def present_tiles(present):
    levels = present.shape[0]
    spread = present.reshape(levels, 2, 2).transpose(0, 2, 1).astype(F32)
    return jnp.broadcast_to(spread[:, :, None, :, None], (levels, 2, 4, 2, 64)).reshape(levels, 8, 128)


def piece_for(pieces, quarter):
    return lax.dynamic_index_in_dim(pieces, quarter, 0, keepdims=False)


def column_pieces(weights):
    parts = [jnp.concatenate([weights[:, 0, :, 64 * q : 64 * q + 64], weights[:, 1, :, 64 * q : 64 * q + 64]], 2) for q in range(4)]
    return jnp.stack(parts)


def assembled(mine, first, second, far, first_is_next):
    after, before = jnp.where(first_is_next, first, second), jnp.where(first_is_next, second, first)
    return jnp.stack([mine, after, far, before], axis=1).reshape(1024, 128)


def column_product(own, partner, present, columns, start, keep):
    both = jnp.concatenate([own, partner * present], axis=0).astype(BF16)
    turn = lax.dynamic_slice(jnp.concatenate([both, both], axis=1), (jnp.uint32(0), start), (32, 256))
    wide = jnp.where(keep, jnp.concatenate([turn] * 4, axis=1), jnp.zeros((), BF16))
    got = jnp.dot(wide, columns, preferred_element_type=F32)
    got = got[:16, :64] + got[16:, 64:]
    return jnp.concatenate([got[:8], got[8:]], axis=1)


def by_side(received, upper):
    low, high = received[:4].astype(F32).sum(0), received[4:].astype(F32).sum(0)
    return jnp.where(upper, high, low), jnp.where(upper, low, high)


def local(load_vectors, cluster_order, block_present, factors):
    leaves, ranks = lax.axis_size("leaf"), lax.axis_size("rank")
    leaf_bits = leaves.bit_length() - 1
    leaf, rank = lax.axis_index("leaf"), lax.axis_index("rank")
    own = own_columns(load_vectors, cluster_order, rank)
    partner = lax.ppermute(own, "leaf", [(at, at ^ 1 << leaf_bits - 1) for at in range(leaves)])
    uppers = [(leaf >> bit & 1) != 0 for bit in range(leaf_bits - 1)]
    core = leaf & 1
    steps = (jnp.where(core == 0, rank ^ 1, 3 - rank), jnp.where(core == 0, 3 - rank, rank ^ 1))

    def moved_on(pieces, step):
        route = []
        for at in range(leaves):
            for r in range(ranks):
                route.append((at * ranks + r, at * ranks + (r ^ 1 if at & 1 == step else 3 - r)))
        return lax.ppermute(jnp.stack(pieces), ("leaf", "rank"), route)

    early, late = BY_COLUMNS
    pieces = {level: column_pieces(factors[level]) for level in BY_COLUMNS}
    moved = [piece_for(pieces[level], to) for level in BY_COLUMNS for to in (rank, *steps, rank ^ 2)]
    first_is_next = (rank + core & 1) == 0
    tiles = present_tiles(block_present)
    partner, tiles, block_present, *rest = lax.optimization_barrier((partner, tiles, block_present, *moved, *uppers))
    of_early, of_late, uppers = rest[:ranks], rest[ranks : 2 * ranks], rest[2 * ranks :]
    columns = {}

    for level in range(LEVELS):
        bit = leaf_bits - 2 - level
        groups = pair_groups(leaves, ranks, bit) if bit >= 0 else None
        if level in BY_COLUMNS:
            own = column_product(whole_own, whole_partner, rows[level], columns[level], start, keep)
            if bit >= 0:
                partner = lax.ppermute(own.astype(BF16), "leaf", [(at, at ^ 1 << bit) for at in range(leaves)])
                partner = partner.astype(F32)
            else:
                partner = turned(own)
            continue
        part, factors = lax.optimization_barrier(
            (product(own, partner, tiles[level], factors[level].reshape(512, 256)), factors)
        )
        if level == 1:
            rows = [jnp.repeat(block_present[at].astype(F32), 4)[:, None] for at in BY_COLUMNS]
            keep = jnp.arange(32)[:, None] // 4 % 4 == jnp.arange(1024)[None, :] // 256
            part, first_is_next, start, keep, *rows = lax.optimization_barrier(
                (part, first_is_next, (64 * rank).astype(jnp.uint32), keep, *rows)
            )
            rows = dict(zip(BY_COLUMNS, rows))
        if level == 0:
            first = moved_on([of_early[1], of_early[3]], 0)
        elif level == 1:
            second = moved_on([of_early[2], first[1]], 1)
        elif level == 2:
            third = moved_on([of_late[1], of_late[3]], 0)
        elif level == 4:
            fourth = moved_on([of_late[2], third[1]], 1)
        if level + 1 == early:
            part, mine, near = lax.optimization_barrier((part, of_early[0], first[0]))
            columns[early] = assembled(mine, near, second[0], second[1], first_is_next)
        elif level + 1 == late:
            part, mine, near = lax.optimization_barrier((part, of_late[0], third[0]))
            columns[late] = assembled(mine, near, fourth[0], fourth[1], first_is_next)
        if level + 1 in BY_COLUMNS:
            sent = jnp.broadcast_to(part.astype(WIDE)[None], (2 * ranks, 16, 256))
            received = lax.all_to_all(sent, ("leaf", "rank"), 0, 0, axis_index_groups=groups, tiled=True)
            whole_own, whole_partner = by_side(received, uppers[bit])
        elif bit >= 0:
            received = lax.all_to_all(chunks(part, 2), ("leaf", "rank"), 0, 0, axis_index_groups=groups, tiled=True)
            own, partner = by_side(received, uppers[bit])
        elif level < LEVELS - 1:
            own = lax.all_to_all(chunks(part, 1), "rank", 0, 0, tiled=True).sum(0)
            partner = turned(own)
        else:
            sent = jnp.broadcast_to(part.astype(WIDE)[None], (ranks, 16, 256))
            whole = lax.all_to_all(sent, "rank", 0, 0, tiled=True).astype(F32).sum(0)
    return put_back(whole, cluster_order)


def solution(mesh):
    in_specs = (
        P("leaf", None, None),
        P("leaf", None),
        P(None, "leaf"),
        P(None, "leaf", None, "rank", None),
    )
    out_specs = P("leaf", None, None)

    return jax.shard_map(local, mesh=mesh, in_specs=in_specs, out_specs=out_specs, check_vma=False)
```

```python
import jax
import jax.numpy as jnp
from jax import lax
from jax.sharding import PartitionSpec as P

LEVELS = 8
F32 = jnp.float32
BF16 = jnp.bfloat16
WIDE = BF16
BY_COLUMNS = (3, 6)


def left_half():
    return lax.broadcasted_iota(jnp.int32, (8, 128), 1) < 64


def turned(tile):
    return jnp.concatenate([tile[:, 64:], tile[:, :64]], axis=1)


def own_columns(loads, order, rank):
    quarter = lax.dynamic_slice_in_dim(order, 64 * rank, 64, 1)
    pick = (jnp.arange(256)[None, :, None] == quarter[:, None, :]).astype(BF16)
    got = jnp.einsum("blc,bco->blo", loads, pick, preferred_element_type=F32)
    return jnp.concatenate([got[:2].reshape(8, 64), got[2:].reshape(8, 64)], axis=1)


def per_block(wide):
    _, columns = wide.shape
    block_of = lax.broadcasted_iota(jnp.int32, wide.shape, 0) // 4 % 4
    part_of = lax.broadcasted_iota(jnp.int32, wide.shape, 1) // (columns // 4)
    return jnp.where(block_of == part_of, wide, jnp.zeros((), wide.dtype))


def product(own, partner, present, weights):
    left = left_half()
    partner = partner * present
    top = jnp.where(left, own, turned(partner))
    bottom = jnp.where(left, turned(own), partner)
    cols = jnp.concatenate([top, bottom], axis=0).astype(BF16)
    wide = per_block(jnp.concatenate([cols] * 4, axis=1))
    return jnp.dot(wide, weights, preferred_element_type=F32)


def chunks(part, copies):
    left = left_half()
    pieces = []
    for at in range(2):
        tile = part[:, 128 * at : 128 * (at + 1)]
        top, bottom = tile[:8], tile[8:]
        pieces += [jnp.where(left, top, turned(bottom)), jnp.where(left, turned(top), bottom)]
    return jnp.broadcast_to(jnp.stack(pieces)[None], (copies, 4, 8, 128)).reshape(copies * 4, 8, 128)


def put_back(state, order):
    high = state.astype(BF16)
    rest = (state - high.astype(F32)).astype(BF16)
    pieces = jnp.concatenate([high, rest], axis=0).reshape(2, 4, 4, 256)
    pick = (jnp.arange(256)[None, :, None] == order[:, None, :]).astype(BF16)
    put = jnp.einsum("pblj,bij->pbli", pieces, pick, preferred_element_type=F32)
    return put[0] + put[1]


def pair_groups(leaves, ranks, bit):
    groups = []
    for leaf in range(leaves):
        if not leaf >> bit & 1:
            groups.append([at * ranks + r for at in (leaf, leaf | 1 << bit) for r in range(ranks)])
    return groups


def present_tiles(present):
    levels = present.shape[0]
    spread = present.reshape(levels, 2, 2).transpose(0, 2, 1).astype(F32)
    return jnp.broadcast_to(spread[:, :, None, :, None], (levels, 2, 4, 2, 64)).reshape(levels, 8, 128)


def piece_for(pieces, quarter):
    return lax.dynamic_index_in_dim(pieces, quarter, 0, keepdims=False)


def column_pieces(weights):
    parts = [jnp.concatenate([weights[:, 0, :, 64 * q : 64 * q + 64], weights[:, 1, :, 64 * q : 64 * q + 64]], 2) for q in range(4)]
    return jnp.stack(parts)


def assembled(mine, first, second, far, first_is_next):
    after, before = jnp.where(first_is_next, first, second), jnp.where(first_is_next, second, first)
    return jnp.stack([mine, after, far, before], axis=1).reshape(1024, 128)


def column_product(own, partner, present, columns, start, keep):
    both = jnp.concatenate([own, partner * present], axis=0).astype(BF16)
    turn = lax.dynamic_slice(jnp.concatenate([both, both], axis=1), (jnp.uint32(0), start), (32, 256))
    wide = jnp.where(keep, jnp.concatenate([turn] * 4, axis=1), jnp.zeros((), BF16))
    got = jnp.dot(wide, columns, preferred_element_type=F32)
    got = got[:16, :64] + got[16:, 64:]
    return jnp.concatenate([got[:8], got[8:]], axis=1)


def by_side(received, upper):
    low, high = received[:4].astype(F32).sum(0), received[4:].astype(F32).sum(0)
    return jnp.where(upper, high, low), jnp.where(upper, low, high)


def local(load_vectors, cluster_order, block_present, factors):
    leaves, ranks = lax.axis_size("leaf"), lax.axis_size("rank")
    leaf_bits = leaves.bit_length() - 1
    leaf, rank = lax.axis_index("leaf"), lax.axis_index("rank")
    own = own_columns(load_vectors, cluster_order, rank)
    partner = lax.ppermute(own, "leaf", [(at, at ^ 1 << leaf_bits - 1) for at in range(leaves)])
    uppers = [(leaf >> bit & 1) != 0 for bit in range(leaf_bits - 1)]
    core = leaf & 1
    steps = (jnp.where(core == 0, rank ^ 1, 3 - rank), jnp.where(core == 0, 3 - rank, rank ^ 1))

    def moved_on(pieces, step):
        route = []
        for at in range(leaves):
            for r in range(ranks):
                route.append((at * ranks + r, at * ranks + (r ^ 1 if at & 1 == step else 3 - r)))
        return lax.ppermute(jnp.stack(pieces), ("leaf", "rank"), route)

    early, late = BY_COLUMNS
    pieces = {level: column_pieces(factors[level]) for level in BY_COLUMNS}
    moved = [piece_for(pieces[level], to) for level in BY_COLUMNS for to in (rank, *steps, rank ^ 2)]
    first_is_next = (rank + core & 1) == 0
    tiles = present_tiles(block_present)
    partner, tiles, block_present, *rest = lax.optimization_barrier((partner, tiles, block_present, *moved, *uppers))
    of_early, of_late, uppers = rest[:ranks], rest[ranks : 2 * ranks], rest[2 * ranks :]
    columns = {}

    for level in range(LEVELS):
        bit = leaf_bits - 2 - level
        groups = pair_groups(leaves, ranks, bit) if bit >= 0 else None
        if level in BY_COLUMNS:
            own = column_product(whole_own, whole_partner, rows[level], columns[level], start, keep)
            if bit >= 0:
                partner = lax.ppermute(own.astype(BF16), "leaf", [(at, at ^ 1 << bit) for at in range(leaves)])
                partner = partner.astype(F32)
            else:
                partner = turned(own)
            continue
        part, factors = lax.optimization_barrier(
            (product(own, partner, tiles[level], factors[level].reshape(512, 256)), factors)
        )
        if level == 1:
            rows = [jnp.repeat(block_present[at].astype(F32), 4)[:, None] for at in BY_COLUMNS]
            keep = jnp.arange(32)[:, None] // 4 % 4 == jnp.arange(1024)[None, :] // 256
            part, first_is_next, start, keep, *rows = lax.optimization_barrier(
                (part, first_is_next, (64 * rank).astype(jnp.uint32), keep, *rows)
            )
            rows = dict(zip(BY_COLUMNS, rows))
        if level == 0:
            first = moved_on([of_early[1], of_early[3]], 0)
        elif level == 1:
            second = moved_on([of_early[2], first[1]], 1)
        elif level == 2:
            third = moved_on([of_late[1], of_late[3]], 0)
        elif level == 4:
            fourth = moved_on([of_late[2], third[1]], 1)
        if level + 1 == early:
            part, mine, near = lax.optimization_barrier((part, of_early[0], first[0]))
            columns[early] = assembled(mine, near, second[0], second[1], first_is_next)
        elif level + 1 == late:
            part, mine, near = lax.optimization_barrier((part, of_late[0], third[0]))
            columns[late] = assembled(mine, near, fourth[0], fourth[1], first_is_next)
        if level + 1 in BY_COLUMNS:
            sent = jnp.broadcast_to(part.astype(WIDE)[None], (2 * ranks, 16, 256))
            received = lax.all_to_all(sent, ("leaf", "rank"), 0, 0, axis_index_groups=groups, tiled=True)
            whole_own, whole_partner = by_side(received, uppers[bit])
        elif bit >= 0:
            received = lax.all_to_all(chunks(part, 2), ("leaf", "rank"), 0, 0, axis_index_groups=groups, tiled=True)
            own, partner = by_side(received, uppers[bit])
        elif level < LEVELS - 1:
            own = lax.all_to_all(chunks(part, 1), "rank", 0, 0, tiled=True).sum(0)
            partner = turned(own)
        else:
            sent = jnp.broadcast_to(part.astype(WIDE)[None], (ranks, 16, 256))
            whole = lax.all_to_all(sent, "rank", 0, 0, tiled=True).astype(F32).sum(0)
    return put_back(whole, cluster_order)


def solution(mesh):
    in_specs = (
        P("leaf", None, None),
        P("leaf", None),
        P(None, "leaf"),
        P(None, "leaf", None, "rank", None),
    )
    out_specs = P("leaf", None, None)

    return jax.shard_map(local, mesh=mesh, in_specs=in_specs, out_specs=out_specs, check_vma=False)
```
